128 devices in a mesh: row: 16 (over y_lo, z, core), col: 8 (over y_hi, x).
Axes of the slice: x: 4, y: 4 (y_hi: 2, y_lo: 2; y = y_hi * 2 + y_lo), z: 4, core: 2. Of those that a mesh axis runs over, the one named last changes fastest.
Arguments:
- policy_rows: bfloat16 [4096, 131072], P(('row', 'col')), may hold values from 0 to 1, as said below
- action_rows: bfloat16 [4096, 16, 8, 1024], P('row', None, 'col'), may hold values from 0 to 1, as said below
- prev_values: float32 [32, 131072], P(None, ('row', 'col')), may hold values from -2000 to 2000
- action_costs: float32 [32, 8, 4096], P(None, None, ('row', 'col')), may hold values from 0 to 2
- policy: int32 [4096], P(('row', 'col')), may hold values from 0 to 7
- target_costs: float32 [32, 4096], P(None, ('row', 'col')), may hold values from 0 to 2
- anchor: int32 [1], replicated, may hold values from 0 to 4095
Outputs:
- relative: float32 [32, 4096], P(None, ('row', 'col'))
- q_values: float32 [32, 4096], P(None, ('row', 'col'))
The draws below stay inside these ranges and needn't reach their ends.
Inputs may be any that keep to these rules, and one draw needn't show every extreme that they name: `policy_rows`: entries are nonnegative transition probabilities, each row sums to about one. `action_rows`: entries are nonnegative transition probabilities, each row sums to about one.
All inputs are finite; a program needn't handle non-finite values.
Results may differ from the reference program's by a relative error of at most 0.0024.
Values may be sent and summed in bfloat16 or wider, within the bound.
A program may use at most 128 MiB of HBM per device.

```python
import jax
import jax.numpy as jnp
from jax import lax

S = 131072
ACTIONS = 8
SCEN = 32
ROW_TILES = 16
COL_TILES = 8
STATE_DEV = 1024
R_PI = 4096
QROWS = 4096


def draw_policy_rows(key, part):
    return jax.random.uniform(key, (R_PI, S), jnp.float32, 0.0, 2.0 / S).astype(jnp.bfloat16)


def draw_action_rows(key, part):
    first, second, third = jax.random.split(key, 3)
    values = jax.random.uniform(first, (QROWS, S), jnp.float32, 0.0, 1.0 / S)
    targets = jax.random.randint(second, (QROWS, 4), 0, R_PI).astype(jnp.int32)
    weights = jax.random.uniform(third, (QROWS, 4), jnp.float32, 0.0625, 0.1875)
    row_ids = jnp.broadcast_to(jnp.arange(QROWS, dtype=jnp.int32)[:, None], (QROWS, 4))
    values = values.at[row_ids, targets].add(weights)
    return values.reshape(QROWS, ROW_TILES, COL_TILES, STATE_DEV).astype(jnp.bfloat16)


def draw_prev_values(key, part):
    spread = 0.8 * jnp.sqrt(jnp.float32(S))
    values = jax.random.normal(key, (SCEN, S), jnp.float32) * spread
    return jnp.clip(values, -2000.0, 2000.0)


def plant(values, own_key, least, largest):
    spot = [jax.random.randint(jax.random.fold_in(own_key, axis), (), 0, length) for axis, length in enumerate(values.shape)]
    longest = values.shape.index(max(values.shape))
    beside = spot[:longest] + [(spot[longest] + 1) % values.shape[longest]] + spot[longest + 1:]
    return values.at[tuple(spot)].set(least).at[tuple(beside)].set(largest)


def steps_of(rng, dims, cuts, smallest, top_value):
    def one(position, shards_of):
        heights = jax.random.uniform(jax.random.fold_in(jax.random.fold_in(rng, 6), position), (shards_of,), jnp.float32, smallest / len(cuts), top_value / len(cuts))
        return jnp.repeat(jnp.exp(heights), dims[position] // shards_of).reshape((-1,) + (1,) * (len(dims) - position - 1))

    level = one(*cuts[0])
    for cut in cuts[1:]:
        level = level * one(*cut)
    return level


def setup_inputs(seed: int = 0) -> dict:
    streams_of = jax.random.split(jax.random.key(seed), 8)
    return {
        "policy_rows": draw_policy_rows(jax.random.fold_in(streams_of[7], 71), 0),
        "action_rows": draw_action_rows(jax.random.fold_in(streams_of[7], 71), 0),
        "prev_values": draw_prev_values(jax.random.fold_in(streams_of[7], 71), 0),
        "action_costs": jnp.clip(2.0 * jax.random.uniform(streams_of[3], (SCEN, ACTIONS, R_PI), jnp.float32) ** steps_of(streams_of[3], (SCEN, ACTIONS, R_PI), ((2, 128),), -0.2, 0.2), 0.0, 2.0),
        "policy": plant(jax.random.randint(streams_of[4], (R_PI,), 0, ACTIONS), jax.random.fold_in(streams_of[4], 1), 0, ACTIONS - 1).astype(jnp.int32),
        "target_costs": jnp.clip(2.0 * jax.random.uniform(streams_of[5], (SCEN, QROWS), jnp.float32) ** steps_of(streams_of[5], (SCEN, QROWS), ((1, 128),), -0.2, 0.2), 0.0, 2.0),
        "anchor": jax.random.randint(streams_of[6], (1,), 0, R_PI).astype(jnp.int32),
    }


def reference(policy_rows, action_rows, prev_values, action_costs, policy, target_costs, anchor):
    prev_bf16 = prev_values.astype(jnp.bfloat16)
    one_hot = (policy[None, :] == jnp.arange(ACTIONS, dtype=jnp.int32)[:, None]).astype(jnp.float32)
    policy_cost = jnp.sum(action_costs * one_hot[None, :, :], axis=1)
    swept_sum = lax.dot_general(prev_bf16, policy_rows, (((1,), (1,)), ((), ())), preferred_element_type=jnp.float32)
    fresh_vals = policy_cost + swept_sum
    gain_value = lax.dynamic_slice_in_dim(fresh_vals, anchor[0].astype(jnp.int32), 1, 1)
    relative = fresh_vals - gain_value
    state_values = jnp.concatenate([relative.astype(jnp.bfloat16), prev_bf16[:, R_PI:]], axis=1)
    flattened = action_rows.reshape(QROWS, S)
    summed_q = lax.dot_general(state_values, flattened, (((1,), (1,)), ((), ())), preferred_element_type=jnp.float32)
    q_values = target_costs + summed_q - gain_value
    return relative, q_values
```

```python
import functools

import jax
import jax.numpy as jnp
from jax import lax
from jax.experimental import pallas as pl
from jax.experimental.pallas import tpu as pltpu
from jax.sharding import PartitionSpec as P

MESH = pl.DeviceIdType.MESH
F32, BF16 = jnp.float32, jnp.bfloat16
STEPS = ((1, 0, 0), (3, 0, 0), (0, 1, 0), (0, 3, 0), (0, 0, 1), (0, 0, 3))
PLAN = (
    (0, 448, 512, 576, 640, 320),
    (384, 64, 128, 192, 256, 704),
    (),
    (),
    (385, 452, 131, 195, 641, 708),
    (1, 67, 129, 579, 268, 323),
    (388, 65, 513, 588, 652, 720),
    (3, 76, 176, 204, 688, 752),
    (4, 112, 514, 578, 657, 327),
    (13, 496, 519, 194, 692, 756),
    (397, 461, 532, 624, 273, 724),
    (404, 497, 564, 241, 308, 380),
    (15, 462, 134, 224, 288, 328),
    (6, 503, 179, 221, 660, 759),
    (399, 508, 180, 637, 664, 352),
    (8, 78, 160, 255, 305, 340),
    (402, 510, 567, 590, 309, 764),
    (25, 502, 551, 253, 281, 727),
    (22, 505, 161, 227, 665, 735),
    (403, 126, 151, 210, 289, 356),
    (5, 123, 164, 254, 676, 763),
    (395, 511, 169, 589, 689, 733),
    (413, 89, 550, 208, 297, 745),
)
LATENCY = 4


def plan_of():
    ready = {(half, 0): 0 for half in range(2)}
    sends = []
    for step, row in enumerate(PLAN):
        line = []
        for entry in row:
            half, rest = divmod(entry, 384)
            way, code = divmod(rest, 64)
            place = (code // 16, code // 4 % 4, code % 4)
            to = tuple((a + b) % 4 for a, b in zip(place, STEPS[way]))
            target = to[0] * 16 + to[1] * 4 + to[2]
            line.append((half, way, code, target))
            ready[half, target] = step + LATENCY
        sends.append(line)
    done = {code: max(ready[0, code], ready[1, code]) for code in range(64)}
    order = sorted(range(64), key=lambda code: (done[code], code))
    slot = {code: n for n, code in enumerate(order)}
    first = max(done[order[4 * g + 3]] - g for g in range(16))
    last = first + 15
    waits = [[] for _ in range(last + 1)]
    for (half, code), when in ready.items():
        if code:
            turn = first + slot[code] // 4
            assert turn >= when, (turn, when)
            uses = [s for s, line in enumerate(sends) for h, _, c, _ in line if (h, c) == (half, code)]
            waits[min(uses + [turn])].append((when, half, slot[code]))
    steps = []
    for step in range(last + 1):
        line = sends[step] if step < len(sends) else []
        steps.append(
            (
                [(h, n) for _, h, n in sorted(waits[step])],
                [(h, way, slot[c], slot[t]) for h, way, c, t in line],
            )
        )
    return order, slot, steps, first


ORDER, SLOT, STEP_PLAN, FIRST = plan_of()


def tile4(x):
    x = x + pltpu.roll(x, 64, 1)
    return x + pltpu.roll(x, 32, 1)


def pack(x, group):
    out = x[0:8]
    for g in range(1, 4):
        out = jnp.where(group[0:8] == g, x[8 * g : 8 * g + 8], out)
    return out


def kernel(
    policy_rows, action_rows, prev, costs, policy, anchor, rel_out, q_out,
    prev_buf, cost_buf, policy_buf, blocks, own_rows, actions, column, first_tile, acc, rest, half_out, half_in,
    packed, gathered, combined, message, arrived,
    in_sem, cost_sem, rows_sem, other_sem, act_sem, recv_sem, col_sem, half_sem, fresh_sem, q_sem, self_sem, send_sem, psend_sem, csend_sem, hsend_sem, fsend_sem, qsend_sem,
):
    row, col = lax.axis_index("row"), lax.axis_index("col")
    core = row % 2
    z = row // 2 % 4
    y_lo = row // 8
    y_hi, x = col // 4, col % 4
    y = y_hi * 2 + y_lo

    def device(x, y, z, core):
        return ((y % 2 * 4 + z) * 2 + core, y // 2 * 4 + x)

    ways = [device((x + a) % 4, (y + b) % 4, (z + c) % 4, core) for a, b, c in STEPS]
    twin = (row + 1 - 2 * core, col)

    load_prev = pltpu.make_async_copy(prev, prev_buf, in_sem.at[0])
    load_prev.start()
    load_costs = pltpu.make_async_copy(costs, cost_buf, cost_sem.at[0])
    load_policy = pltpu.make_async_copy(policy, policy_buf, cost_sem.at[1])
    load_costs.start()
    load_policy.start()

    barrier = pltpu.get_barrier_semaphore()
    for other in ways + [twin]:
        pl.semaphore_signal(barrier, inc=1, device_id=other, device_id_type=MESH)

    def block_of(code, core):
        there = device((x - code // 16) % 4, (y - code // 4 % 4) % 4, (z - code % 4) % 4, core)
        return pl.multiple_of((there[0] * 8 + there[1]) * 1024, 1024)

    def load_rows(n):
        pltpu.make_async_copy(
            policy_rows.at[:, pl.ds(block_of(ORDER[n], core), 1024)], own_rows.at[n, pl.ds(0, 32)], rows_sem.at[n // 4]
        ).start()

    def send_rows(n):
        pltpu.make_async_remote_copy(
            policy_rows.at[:, pl.ds(block_of(ORDER[n], 1 - core), 1024)], own_rows.at[n, pl.ds(32, 32)],
            psend_sem.at[0], other_sem.at[n // 4], device_id=twin, device_id_type=MESH,
        ).start()

    load_prev.wait()
    blocks[0] = prev_buf[...].astype(BF16)
    pl.semaphore_wait(barrier, 7)

    def send_block(half, way, source, target):
        pltpu.make_async_remote_copy(
            blocks.at[source, pl.ds(16 * half, 16)], blocks.at[target, pl.ds(16 * half, 16)],
            send_sem.at[0], recv_sem.at[half * 64 + target], device_id=ways[way], device_id_type=MESH,
        ).start()

    def wait_block(half, n):
        there = blocks.at[n, pl.ds(16 * half, 16)]
        pltpu.make_async_copy(there, there, recv_sem.at[half * 64 + n]).wait()

    def act_copy(n):
        return pltpu.make_async_copy(
            action_rows.at[pl.ds(n * 32, 32)], actions.at[pl.ds(n * 32, 32)], act_sem.at[n]
        )

    acc[...] = jnp.zeros_like(acc)
    lanes = lax.broadcasted_iota(jnp.int32, (64, 128), 1)
    group = lanes // 32

    def column_copies(n):
        y_other, z_other = n // 4, n % 4
        code = (y_lo - y_other + 4) % 4 * 4 + (z - z_other + 4) % 4
        return code, (y_other * 4 + z_other) * 2 + core

    def slot_of(code):
        out = 0
        for c in (0, 1, 2, 3, 4, 5, 6, 7, 12, 13, 14, 15):
            out = out + jnp.where(code == c, SLOT[c], 0)
        return out

    column_step = 1 + max(
        s for s, (waits, _) in enumerate(STEP_PLAN) for _, n in waits if ORDER[n] // 16 == 0 and ORDER[n] // 4 % 4 != 2
    )

    def forward_column():
        for n in range(8):
            code, place = column_copies(n)
            n_slot = slot_of(code)
            pltpu.make_async_remote_copy(
                blocks.at[n_slot], column.at[place], csend_sem.at[0], col_sem.at[1], device_id=twin, device_id_type=MESH
            ).start()
            pltpu.make_async_copy(blocks.at[n_slot], column.at[place], col_sem.at[0]).start()

    def wait_column():
        eight = column.at[pl.ds(0, 8)]
        pltpu.make_async_copy(eight, eight, col_sem.at[0]).wait()
        pltpu.make_async_copy(eight, eight, col_sem.at[1]).wait()

    def policy_group(g):
        mine = own_rows.at[pl.ds(4 * g, 4), pl.ds(0, 32)]
        pltpu.make_async_copy(mine, mine, rows_sem.at[g]).wait()
        twins = own_rows.at[pl.ds(4 * g, 4), pl.ds(32, 32)]
        pltpu.make_async_copy(twins, twins, other_sem.at[g]).wait()
        left = own_rows[pl.ds(4 * g, 4)].reshape(256, 1024)
        right = blocks[pl.ds(4 * g, 4)].reshape(128, 1024)
        acc[...] += lax.dot_general(left, right, (((1,), (1,)), ((), ())), preferred_element_type=F32)

    has_fresh = col < 4

    def action_chunk(n):
        @pl.when(n % 2 == 0)
        def _():
            act_copy(n // 2).wait()

        chunk = actions[pl.ds(16 * n, 16)].reshape(256, 1024)
        values = column[...].reshape(512, 1024)
        out = lax.dot_general(chunk, values, (((1,), (1,)), ((), ())), preferred_element_type=F32)
        out = out.reshape(16, 16, 512)
        here = lax.broadcasted_iota(jnp.int32, (16, 512), 0)
        there = lax.broadcasted_iota(jnp.int32, (16, 512), 1) // 32
        keep = (here == there) & ((there > 0) | jnp.logical_not(has_fresh))
        out = jnp.sum(jnp.where(keep[None], out, 0.0), axis=1)
        out = out[:, 0:128] + out[:, 128:256] + (out[:, 256:384] + out[:, 384:512])
        rest[pl.ds(16 * n, 16)] = tile4(out)

        @pl.when(has_fresh)
        def _():
            pick = (
                lax.broadcasted_iota(jnp.int32, (16, 256), 1) == 16 * lax.broadcasted_iota(jnp.int32, (16, 256), 0)
            ).astype(BF16)
            first_tile[pl.ds(16 * n, 16)] = jnp.dot(pick, chunk, preferred_element_type=F32).astype(BF16)

    last = len(STEP_PLAN) - 1
    chunk_first = max(column_step + 1, 0)
    n_steps = max(last + 1, chunk_first + 16)

    @pl.loop(0, n_steps)
    def _(t):
        for s, (waits, sends) in enumerate(STEP_PLAN):

            @pl.when(t == s)
            def _(s=s, waits=waits, sends=sends):
                for half, n in waits:
                    wait_block(half, n)
                for send in sends:
                    send_block(*send)
                if s == 0:
                    for n in range(64):
                        load_rows(n)
                        send_rows(n)
                    for n in range(8):
                        act_copy(n).start()
                if s == column_step:
                    forward_column()

        @pl.when(t == column_step + 1)
        def _():
            wait_column()

        @pl.when((t >= FIRST) & (t < FIRST + 16))
        def _():
            policy_group(t - FIRST)

        @pl.when((t >= chunk_first) & (t < chunk_first + 16))
        def _():
            action_chunk(t - chunk_first)

    load_costs.wait()
    load_policy.wait()
    chosen = policy_buf[...][:, None, :] == lax.broadcasted_iota(jnp.int32, (1, 8, 32), 1)
    cost = jnp.sum(jnp.where(chosen, cost_buf[...], 0.0), axis=1)
    cost = jnp.concatenate([cost] * 4, axis=0).T

    total = jnp.zeros((64, 128), F32)
    for b in range(4):
        total = total + jnp.where(group == b, acc[64 * b : 64 * b + 64, :], 0.0)
    total = tile4(total)
    half_out[...] = pack(total[32:64], group)
    mine = pack(total[0:32] + cost, group)
    swap = pltpu.make_async_remote_copy(
        half_out, half_in, hsend_sem.at[0], half_sem.at[0], device_id=twin, device_id_type=MESH
    )
    swap.start()
    swap.wait_recv()
    packed[...] = mine + half_in[...]

    place = row % 4 * 8 + col
    target_col = row // 4
    for r in range(16):
        local = (row == r) & (col == target_col)

        @pl.when(local)
        def _():
            pltpu.make_async_copy(packed, gathered.at[place], fresh_sem.at[0]).start()

        @pl.when(jnp.logical_not(local))
        def _(r=r):
            pltpu.make_async_remote_copy(
                packed, gathered.at[place], fsend_sem.at[0], fresh_sem.at[0],
                device_id=(r, target_col), device_id_type=MESH,
            ).start()

    small = group[0:8]

    @pl.when(has_fresh)
    def _():
        pltpu.make_async_copy(gathered, gathered, fresh_sem.at[0]).wait()
        for n in range(32):
            line = gathered[n]
            for g in range(4):
                full = tile4(jnp.where(small == g, line, 0.0))
                high = full.astype(BF16).astype(F32)
                mid = (full - high).astype(BF16).astype(F32)
                low = full - high - mid
                parts = jnp.where(small == 0, high, jnp.where(small == 1, mid, jnp.where(small == 2, low, 1.0)))
                combined[32 * n + 8 * g : 32 * n + 8 * g + 8] = parts.astype(BF16)
        late = jnp.dot(first_tile[...], combined[...], preferred_element_type=F32)
        wide = lax.broadcasted_iota(jnp.int32, (256, 128), 1) // 32
        values = rest[...] + tile4(jnp.where(wide < 3, late, 0.0))
        weights = tile4(jnp.where(wide == 3, late, 0.0))
        state = (
            col * 1024 + lax.broadcasted_iota(jnp.int32, (32, 8, 128), 0) * 32
            + lax.broadcasted_iota(jnp.int32, (32, 8, 128), 2) // 32 * 8
            + lax.broadcasted_iota(jnp.int32, (32, 8, 128), 1)
        )
        gain = jnp.sum(jnp.where(state == anchor[0], gathered[...], 0.0), axis=0)
        gain = tile4(jnp.broadcast_to(jnp.sum(gain, axis=0, keepdims=True), (8, 128)))
        for c in range(8):
            message[c, 0:8] = pack(values[32 * c : 32 * c + 32], small)
            message[c, 8:16] = pack(weights[32 * c : 32 * c + 32], small)
            message[c, 16:24] = gain

    @pl.when(jnp.logical_not(has_fresh))
    def _():
        for c in range(8):
            message[c, 0:8] = pack(rest[32 * c : 32 * c + 32], small)
            message[c, 8:24] = jnp.zeros((16, 128), F32)

    for c in range(8):
        local = col == c

        @pl.when(local)
        def _(c=c):
            pltpu.make_async_copy(message.at[c], arrived.at[col], q_sem.at[0]).start()

        @pl.when(jnp.logical_not(local))
        def _(c=c):
            pltpu.make_async_remote_copy(
                message.at[c], arrived.at[col], qsend_sem.at[0], q_sem.at[0], device_id=(row, c), device_id_type=MESH
            ).start()
    pltpu.make_async_copy(arrived, arrived, q_sem.at[0]).wait()
    total = arrived[0]
    for c in range(1, 8):
        total = total + arrived[c]
    gain = total[16:24]
    rel_out[...] = packed[...] - gain
    q_out[...] = total[0:8] - gain * total[8:16] - gain

    sent = blocks.at[pl.ds(0, 63)]
    pltpu.make_async_copy(sent, sent, send_sem.at[0]).wait()
    given = own_rows.at[:, pl.ds(32, 32)]
    pltpu.make_async_copy(given, given, psend_sem.at[0]).wait()
    eight = column.at[pl.ds(0, 8)]
    pltpu.make_async_copy(eight, eight, csend_sem.at[0]).wait()
    swap.wait_send()

    @pl.when(col == target_col)
    def _():
        part = gathered.at[pl.ds(0, 15)]
        pltpu.make_async_copy(part, part, fsend_sem.at[0]).wait()

    @pl.when(col != target_col)
    def _():
        part = gathered.at[pl.ds(0, 16)]
        pltpu.make_async_copy(part, part, fsend_sem.at[0]).wait()

    part = arrived.at[pl.ds(0, 7)]
    pltpu.make_async_copy(part, part, qsend_sem.at[0]).wait()


def local(policy_rows, action_rows, prev_values, action_costs, policy, target_costs, anchor):
    any_spec = pl.BlockSpec(memory_space=pl.ANY)
    dma = pltpu.SemaphoreType.DMA
    relative, values = pl.pallas_call(
        kernel,
        out_shape=[jax.ShapeDtypeStruct((8, 128), F32)] * 2,
        in_specs=[any_spec] * 5 + [pl.BlockSpec(memory_space=pltpu.SMEM)],
        out_specs=[pl.BlockSpec(memory_space=pltpu.VMEM)] * 2,
        scratch_shapes=[
            pltpu.VMEM((32, 1024), F32),
            pltpu.VMEM((32, 8, 32), F32),
            pltpu.VMEM((1, 32), jnp.int32),
            pltpu.VMEM((64, 32, 1024), BF16),
            pltpu.VMEM((64, 64, 1024), BF16),
            pltpu.VMEM((256, 16, 1024), BF16),
            pltpu.VMEM((16, 32, 1024), BF16),
            pltpu.VMEM((256, 1024), BF16),
            pltpu.VMEM((256, 128), F32),
            pltpu.VMEM((256, 128), F32),
            pltpu.VMEM((8, 128), F32),
            pltpu.VMEM((8, 128), F32),
            pltpu.VMEM((8, 128), F32),
            pltpu.VMEM((32, 8, 128), F32),
            pltpu.VMEM((1024, 128), BF16),
            pltpu.VMEM((8, 24, 128), F32),
            pltpu.VMEM((8, 24, 128), F32),
            dma((1,)), dma((2,)), dma((16,)), dma((16,)), dma((8,)), dma((128,)), dma((2,)), dma((1,)), dma((1,)),
            dma((1,)), dma((1,)), dma((1,)), dma((1,)), dma((1,)), dma((1,)), dma((1,)), dma((1,)),
        ],
        compiler_params=pltpu.CompilerParams(
            collective_id=0, has_side_effects=True, vmem_limit_bytes=60 * 1024 * 1024
        ),
    )(
        policy_rows,
        action_rows.reshape(action_rows.shape[0], 16, 1024),
        prev_values,
        action_costs,
        policy.reshape(1, 32),
        anchor,
    )

    def spread(x):
        return x.reshape(8, 4, 32).transpose(2, 1, 0).reshape(32, 32)

    return spread(relative), spread(values) + target_costs


def solution(mesh):
    in_specs = (
        P(("row", "col"), None),
        P("row", None, "col", None),
        P(None, ("row", "col")),
        P(None, None, ("row", "col")),
        P(("row", "col")),
        P(None, ("row", "col")),
        P(),
    )
    out_specs = (P(None, ("row", "col")), P(None, ("row", "col")))
    return jax.shard_map(local, mesh=mesh, in_specs=in_specs, out_specs=out_specs, check_vma=False)
```

```python
import functools

import jax
import jax.numpy as jnp
from jax import lax
from jax.experimental import pallas as pl
from jax.experimental.pallas import tpu as pltpu
from jax.sharding import PartitionSpec as P

MESH = pl.DeviceIdType.MESH
F32, BF16 = jnp.float32, jnp.bfloat16
STEPS = ((1, 0, 0), (3, 0, 0), (0, 1, 0), (0, 3, 0), (0, 0, 1), (0, 0, 3))
ORDER = (
    0, 1, 3, 4, 12, 16, 48, 15, 60, 5, 13, 2, 7, 8, 20, 51, 28, 19, 49, 52, 6, 14, 63, 29, 35, 55, 9, 36, 44, 53, 50,
    61, 18, 24, 11, 10, 22, 30, 45, 47, 54, 57, 40, 34, 62, 37, 23, 39, 59, 25, 32, 21, 17, 27, 43, 26, 33, 46, 58, 56,
    31, 38, 41, 42,
)
EVENTS = (
    5101, 9198, 17387, 25580, 33769, 46058, 1005, 13294, 21483, 29676, 37865, 41962, 54262, 107511, 136178, 95216,
    70684, 123892, 1, 9274, 4, 1272, 17457, 66, 29807, 33843, 42223, 9456, 5241, 25650, 3, 1206, 17589, 69, 30008, 65,
    21553, 37939, 67, 46260, 70, 13722, 68, 29941, 46455, 2, -1, 38266, 5, 42297, 13499, 6, 17787, 74, 38525, 15, 10176,
    5759, 18369, 78, 6019, 30338, 22409, 72, 46590, 26558, 18, 10400, 18565, 9, 34364, 1627, 71, 30154, 16, 34815,
    17986, 7, 42429, 11, 1736, 38407, -2, 8, 9732, 73, 38460, 13893, 76, 14081, 42950, 10, 75, -3, 114, 49280, 32900,
    14, 1923, 9863, 5832, 26633, 79, 47046, 12, 13, 77, -4, 24, 18967, 87, 6606, 31193, 39373, 1508, 26058, 46998, 91,
    23250, 39637, 10083, 85, 31051, 80, 17, 81, 82, 19, 83, -5, 86, 14735, 20, 18699, 43539, 97, 48221, 98, 15512,
    27151, 84, 6412, 21, -201, 29, 35664, 32, 19468, 19281, 22, 43412, 90, 14993, 28, 27410, 23, 35277, 2510, 88, 47635,
    -6, 11093, 1814, 23063, 27032, 25, 89, 26, 27, -7, 95, 39892, 56, 45594, 93, 39760, 113, 8294, 47, 20446, 18908,
    101, 7521, 41055, 33, 35929, 106, 48798, 92, 30, 94, 31, -8, -101, 109, 16219, 32608, 60, 29469, 35, 3295, 14179,
    117, 24932, -102, 40, 11813, 20002, 100, 7461, 96, 34, 99, -9, 112, 49186, 38, 36257, 28070, 36, 37, 102, 39, 103,
    -10, -103, 126, 41895, 54, 45479, -104, 104, 41, 105, 42, 43, 107, -11, 44, 108, 45, 46, 110, 111, -12, 48, 49, 50,
    51, 115, -13, -105, 52, 116, 53, 118, 55, 119, -14, 120, 57, 121, 58, 122, 59, 123, -15, 124, 61, 125, 62, 63, 127,
    -16,
)
CHUNKS_DURING = 5
CHUNKS = 8


def hops_of():
    hops = [STEPS[i] for i in range(6)]
    for a in range(6):
        for b in range(a + 1, 6):
            if a // 2 != b // 2:
                hops.append(tuple((p + q) % 4 for p, q in zip(STEPS[a], STEPS[b])))
    return hops


HOPS = hops_of()


def tile4(x):
    x = x + pltpu.roll(x, 64, 1)
    return x + pltpu.roll(x, 32, 1)


def lane_group(rows):
    return lax.broadcasted_iota(jnp.int32, (rows, 128), 1) // 32


def kernel(
    policy_rows, action_rows, prev, costs, policy, targets, anchor, rel_out, q_out,
    prev_buf, cost_buf, policy_buf, target_buf, anchor_buf, blocks, own_rows, actions, column, first_tile, acc, rest,
    cost_part, half_out, half_in, fresh, parts, combined, message, arrived,
    in_sem, rows_sem, other_sem, act_sem, recv_sem, col_sem, half_sem, fresh_sem, q_sem,
    send_sem, psend_sem, csend_sem, hsend_sem, fsend_sem, qsend_sem,
):
    row, col = lax.axis_index("row"), lax.axis_index("col")
    core = row % 2
    z = row // 2 % 4
    y_lo = row // 8
    y_hi, x = col // 4, col % 4
    y = y_hi * 2 + y_lo

    def device(x, y, z, core):
        return ((y % 2 * 4 + z) * 2 + core, y // 2 * 4 + x)

    ways = [device((x + a) % 4, (y + b) % 4, (z + c) % 4, core) for a, b, c in HOPS]
    twin = (row + 1 - 2 * core, col)

    barrier = pltpu.get_barrier_semaphore()
    for other in ways + [twin]:
        pl.semaphore_signal(barrier, inc=1, device_id=other, device_id_type=MESH)

    load_prev = pltpu.make_async_copy(prev, prev_buf, in_sem.at[0])
    load_prev.start()

    def block_of(code, core):
        there = device((x - code // 16) % 4, (y - code // 4 % 4) % 4, (z - code % 4) % 4, core)
        return pl.multiple_of((there[0] * 8 + there[1]) * 1024, 1024)

    for n in range(64):
        pltpu.make_async_copy(
            policy_rows.at[:, pl.ds(block_of(ORDER[n], core), 1024)], own_rows.at[n, pl.ds(0, 32)], rows_sem.at[n // 4]
        ).start()

    small_loads = [
        pltpu.make_async_copy(source, target, in_sem.at[n + 1])
        for n, (source, target) in enumerate(
            ((costs, cost_buf), (policy, policy_buf), (targets, target_buf), (anchor, anchor_buf))
        )
    ]
    for copy in small_loads:
        copy.start()

    load_prev.wait()
    blocks[0] = prev_buf[...].astype(BF16)
    pl.semaphore_wait(barrier, 19)

    def wait_for(ref, sem):
        pltpu.make_async_copy(ref, ref, sem).wait()

    def send_rows():
        for n in range(64):
            pltpu.make_async_remote_copy(
                policy_rows.at[:, pl.ds(block_of(ORDER[n], 1 - core), 1024)], own_rows.at[n, pl.ds(32, 32)],
                psend_sem.at[0], other_sem.at[n // 4], device_id=twin, device_id_type=MESH,
            ).start()
        for n in range(CHUNKS):
            half, part = n % 2, n // 2
            pltpu.make_async_copy(
                action_rows.at[pl.ds(64 * part, 64), pl.ds(8 * half, 8)], actions.at[half, pl.ds(64 * part, 64)],
                act_sem.at[n],
            ).start()

    def part_cost():
        for copy in small_loads:
            copy.wait()
        chosen = policy_buf[...][:, None, :] == lax.broadcasted_iota(jnp.int32, (1, 8, 32), 1)
        cost = jnp.sum(jnp.where(chosen, cost_buf[...], 0.0), axis=1)
        cost_part[...] = jnp.concatenate([cost] * 4, axis=0).T

    def send_block(half, hop, source, target):
        pltpu.make_async_remote_copy(
            blocks.at[source, pl.ds(16 * half, 16)], blocks.at[target, pl.ds(16 * half, 16)],
            send_sem.at[0], recv_sem.at[half * 64 + target], device_id=ways[hop], device_id_type=MESH,
        ).start()

    slot = {code: n for n, code in enumerate(ORDER)}

    def forward_column():
        for n in range(8):
            y_other, z_other = n // 4, n % 4
            code = (y_lo - y_other + 4) % 4 * 4 + (z - z_other + 4) % 4
            where = 0
            for c in range(16):
                if c // 4 != 2:
                    where = where + jnp.where(code == c, slot[c], 0)
            place = n * 2 + core
            pltpu.make_async_remote_copy(
                blocks.at[where], column.at[place], csend_sem.at[0], col_sem.at[1], device_id=twin, device_id_type=MESH
            ).start()
            pltpu.make_async_copy(blocks.at[where], column.at[place], col_sem.at[0]).start()

    def policy_group(g):
        wait_for(own_rows.at[pl.ds(4 * g, 4), pl.ds(0, 32)], rows_sem.at[g])
        wait_for(own_rows.at[pl.ds(4 * g, 4), pl.ds(32, 32)], other_sem.at[g])
        left = own_rows[4 * g : 4 * g + 4].reshape(256, 1024)
        right = blocks[4 * g : 4 * g + 4].reshape(128, 1024)
        out = lax.dot_general(left, right, (((1,), (1,)), ((), ())), preferred_element_type=F32)
        acc[...] = out if g == 0 else acc[...] + out

    has_fresh = col < 4

    def action_chunk(n):
        half, part = n % 2, n // 2
        if n == 0:
            eight = column.at[pl.ds(0, 8)]
            wait_for(eight, col_sem.at[0])
            wait_for(eight, col_sem.at[1])
        here = pl.ds(64 * part, 64)
        wait_for(actions.at[half, here], act_sem.at[n])
        chunk = actions[half, here].reshape(512, 1024)
        values = column[8 * half : 8 * half + 8].reshape(256, 1024)
        out = lax.dot_general(chunk, values, (((1,), (1,)), ((), ())), preferred_element_type=F32)
        out = out.reshape(64, 8, 256)
        mine = lax.broadcasted_iota(jnp.int32, (8, 256), 0)
        theirs = lax.broadcasted_iota(jnp.int32, (8, 256), 1) // 32
        keep = mine == theirs
        if half == 0:
            keep = keep & ((theirs > 0) | jnp.logical_not(has_fresh))
        out = jnp.where(keep[None], out, 0.0)
        out = jnp.sum(out[:, :, 0:128] + out[:, :, 128:256], axis=1)
        if half == 0:
            rest[here] = out

            @pl.when(has_fresh)
            def _():
                pick = (
                    lax.broadcasted_iota(jnp.int32, (64, 512), 1) == 8 * lax.broadcasted_iota(jnp.int32, (64, 512), 0)
                ).astype(BF16)
                first_tile[here] = jnp.dot(pick, chunk, preferred_element_type=F32).astype(BF16)
        else:
            rest[here] = jnp.where(lane_group(64) == 0, tile4(rest[here] + out), 0.0)

    sent = 0
    for event in EVENTS:
        if event >= 1000:
            event, target = divmod(event - 1000, 64)
            event, source = divmod(event, 64)
            send_block(event % 2, event // 2, source, target)
            sent += 1
            if sent == 12:
                send_rows()
                part_cost()
        elif event >= 0:
            half, n = divmod(event, 64)
            wait_for(blocks.at[n, pl.ds(16 * half, 16)], recv_sem.at[event])
        elif event > -100:
            policy_group(-1 - event)
        elif event > -200:
            action_chunk(-101 - event)
        else:
            forward_column()

    group = lane_group(64)
    total = jnp.where(group == 0, acc[0:64, :], 0.0)
    for b in range(1, 4):
        total = jnp.where(group == b, acc[64 * b : 64 * b + 64, :], total)
    total = tile4(total)
    half_out[...] = total[32:64]
    swap = pltpu.make_async_remote_copy(
        half_out, half_in, hsend_sem.at[0], half_sem.at[0], device_id=twin, device_id_type=MESH
    )
    swap.start()
    mine = total[0:32] + cost_part[...]
    swap.wait_recv()
    mine = mine + half_in[...]
    fresh[...] = mine
    group = lane_group(32)
    high = mine.astype(BF16).astype(F32)
    mid = (mine - high).astype(BF16).astype(F32)
    low = mine - high - mid
    parts[...] = jnp.where(
        group == 0, high, jnp.where(group == 1, mid, jnp.where(group == 2, low, 1.0))
    ).astype(BF16)

    place = row % 4 * 8 + col
    target_col = row // 4
    is_target = col == target_col
    for k in range(1, 16):
        pltpu.make_async_remote_copy(
            parts, combined.at[place], fsend_sem.at[0], fresh_sem.at[0],
            device_id=((row + k) % 16, target_col), device_id_type=MESH,
        ).start()

    @pl.when(is_target)
    def _():
        pltpu.make_async_copy(parts, combined.at[place], fresh_sem.at[0]).start()

    @pl.when(jnp.logical_not(is_target))
    def _():
        pltpu.make_async_remote_copy(
            parts, combined.at[place], fsend_sem.at[0], fresh_sem.at[0],
            device_id=(row, target_col), device_id_type=MESH,
        ).start()

    for n in range(CHUNKS_DURING, CHUNKS):
        action_chunk(n)

    @pl.when(has_fresh)
    def _():
        wait_for(combined, fresh_sem.at[0])
        states = col * 1024 + lax.broadcasted_iota(jnp.int32, (8, 1024), 1)
        chosen = (states == anchor_buf[...]).astype(BF16)
        values = combined[...].reshape(1024, 128)
        gain = jnp.dot(chosen, values, preferred_element_type=F32)
        late = jnp.dot(first_tile[...], values, preferred_element_type=F32) + rest[...]
        for c in range(8):
            message[c, 0:32] = late[32 * c : 32 * c + 32]
            message[c, 32:40] = gain

    @pl.when(jnp.logical_not(has_fresh))
    def _():
        for c in range(8):
            message[c, 0:32] = rest[32 * c : 32 * c + 32]
            message[c, 32:40] = jnp.zeros((8, 128), F32)

    for k in range(1, 8):
        other = (col + k) % 8
        pltpu.make_async_remote_copy(
            message.at[other], arrived.at[k - 1], qsend_sem.at[0], q_sem.at[0],
            device_id=(row, other), device_id_type=MESH,
        ).start()
    total = message[col]
    wait_for(arrived, q_sem.at[0])
    for k in range(7):
        total = total + arrived[k]
    gain = tile4(jnp.where(lane_group(8) < 3, total[32:40], 0.0))[0:1]
    total = total[0:32]
    values = tile4(jnp.where(group < 3, total, 0.0))
    weights = tile4(jnp.where(group == 3, total, 0.0))
    both = jnp.where(group == 0, fresh[...] - gain, values - gain * weights - gain).T
    rel_out[...] = both[0:32]
    q_out[...] = both[32:64] + target_buf[...]

    wait_for(blocks.at[pl.ds(0, 63)], send_sem.at[0])
    wait_for(own_rows.at[:, pl.ds(32, 32)], psend_sem.at[0])
    wait_for(column.at[pl.ds(0, 8)], csend_sem.at[0])
    swap.wait_send()

    @pl.when(is_target)
    def _():
        wait_for(combined.at[pl.ds(0, 15)], fsend_sem.at[0])

    @pl.when(jnp.logical_not(is_target))
    def _():
        wait_for(combined.at[pl.ds(0, 16)], fsend_sem.at[0])

    wait_for(arrived, qsend_sem.at[0])


def local(policy_rows, action_rows, prev_values, action_costs, policy, target_costs, anchor):
    any_spec = pl.BlockSpec(memory_space=pl.ANY)
    dma = pltpu.SemaphoreType.DMA
    return pl.pallas_call(
        kernel,
        out_shape=[jax.ShapeDtypeStruct((32, 32), F32)] * 2,
        in_specs=[any_spec] * 7,
        out_specs=[pl.BlockSpec(memory_space=pltpu.VMEM)] * 2,
        scratch_shapes=[
            pltpu.VMEM((32, 1024), F32),
            pltpu.VMEM((32, 8, 32), F32),
            pltpu.VMEM((1, 32), jnp.int32),
            pltpu.VMEM((32, 32), F32),
            pltpu.VMEM((1, 1), jnp.int32),
            pltpu.VMEM((64, 32, 1024), BF16),
            pltpu.VMEM((64, 64, 1024), BF16),
            pltpu.VMEM((2, 256, 8, 1024), BF16),
            pltpu.VMEM((16, 32, 1024), BF16),
            pltpu.VMEM((256, 1024), BF16),
            pltpu.VMEM((256, 128), F32),
            pltpu.VMEM((256, 128), F32),
            pltpu.VMEM((32, 128), F32),
            pltpu.VMEM((32, 128), F32),
            pltpu.VMEM((32, 128), F32),
            pltpu.VMEM((32, 128), F32),
            pltpu.VMEM((32, 128), BF16),
            pltpu.VMEM((32, 32, 128), BF16),
            pltpu.VMEM((8, 40, 128), F32),
            pltpu.VMEM((7, 40, 128), F32),
            dma((5,)), dma((16,)), dma((16,)), dma((8,)), dma((128,)), dma((2,)), dma((1,)), dma((1,)), dma((1,)),
            dma((1,)), dma((1,)), dma((1,)), dma((1,)), dma((1,)), dma((1,)),
        ],
        compiler_params=pltpu.CompilerParams(
            collective_id=0, has_side_effects=True, vmem_limit_bytes=60 * 1024 * 1024
        ),
    )(
        policy_rows,
        action_rows.reshape(action_rows.shape[0], 16, 1024),
        prev_values,
        action_costs,
        policy.reshape(1, 32),
        target_costs,
        anchor.reshape(1, 1),
    )


def solution(mesh):
    in_specs = (
        P(("row", "col"), None),
        P("row", None, "col", None),
        P(None, ("row", "col")),
        P(None, None, ("row", "col")),
        P(("row", "col")),
        P(None, ("row", "col")),
        P(),
    )
    out_specs = (P(None, ("row", "col")), P(None, ("row", "col")))
    return jax.shard_map(local, mesh=mesh, in_specs=in_specs, out_specs=out_specs, check_vma=False)
```

```python
import functools

import jax
import jax.numpy as jnp
from jax import lax
from jax.experimental import pallas as pl
from jax.experimental.pallas import tpu as pltpu
from jax.sharding import PartitionSpec as P

MESH = pl.DeviceIdType.MESH
F32, BF16 = jnp.float32, jnp.bfloat16
STEPS = ((1, 0, 0), (3, 0, 0), (0, 1, 0), (0, 3, 0), (0, 0, 1), (0, 0, 3))
ORDER = (
    0, 1, 3, 4, 12, 16, 48, 15, 60, 5, 13, 2, 7, 8, 20, 51, 28, 19, 49, 52, 6, 14, 63, 29, 35, 55, 9, 36, 44, 53, 50,
    61, 18, 24, 11, 10, 22, 30, 45, 47, 54, 57, 40, 34, 62, 37, 23, 39, 59, 25, 32, 21, 17, 27, 43, 26, 33, 46, 58, 56,
    31, 38, 41, 42,
)
EVENTS = (
    5101, 9198, 17387, 25580, 33769, 46058, 1005, 13294, 21483, 29676, 37865, 41962, 54262, 107511, 136178, 95216,
    70684, 123892, 1, 9274, 4, 1272, 17457, 66, 29807, 33843, 42223, 9456, 5241, 25650, 3, 1206, 17589, 69, 30008, 65,
    21553, 37939, 67, 46260, 70, 13722, 68, 29941, 46455, 2, -1, 38266, 5, 42297, 13499, 6, 17787, 74, 38525, 15, 10176,
    5759, 18369, 78, 6019, 30338, 22409, 72, 46590, 26558, 18, 10400, 18565, 9, 34364, 1627, 71, 30154, 16, 34815,
    17986, 7, 42429, 11, 1736, 38407, -2, 8, 9732, 73, 38460, 13893, 76, 14081, 42950, 10, 75, -3, 114, 49280, 32900,
    14, 1923, 9863, 5832, 26633, 79, 47046, 12, 13, 77, -4, 24, 18967, 87, 6606, 31193, 39373, 1508, 26058, 46998, 91,
    23250, 39637, 10083, 85, 31051, 80, 17, 81, 82, 19, 83, -5, 86, 14735, 20, 18699, 43539, 97, 48221, 98, 15512,
    27151, 84, 6412, 21, -201, 29, 35664, 32, 19468, 19281, 22, 43412, 90, 14993, 28, 27410, 23, 35277, 2510, 88, 47635,
    -6, 11093, 1814, 23063, 27032, 25, 89, 26, 27, -7, 95, 39892, 56, 45594, 93, 39760, 113, 8294, 47, 20446, 18908,
    101, 7521, 41055, 33, 35929, 106, 48798, 92, 30, 94, 31, -8, -101, 109, 16219, 32608, 60, 29469, 35, 3295, 14179,
    117, 24932, -102, 40, 11813, 20002, 100, 7461, 96, 34, 99, -9, 112, 49186, 38, 36257, 28070, 36, 37, 102, 39, 103,
    -10, -103, 126, 41895, 54, 45479, -104, 104, 41, 105, 42, 43, 107, -11, 44, 108, 45, 46, 110, 111, -12, 48, 49, 50,
    51, 115, -13, -105, 52, 116, 53, 118, 55, 119, -14, 120, 57, 121, 58, 122, 59, 123, -15, 124, 61, 125, 62, 63, 127,
    -16,
)
CHUNKS_DURING = 5
CHUNKS = 8


def hops_of():
    hops = [STEPS[i] for i in range(6)]
    for a in range(6):
        for b in range(a + 1, 6):
            if a // 2 != b // 2:
                hops.append(tuple((p + q) % 4 for p, q in zip(STEPS[a], STEPS[b])))
    return hops


HOPS = hops_of()


def tile4(x):
    x = x + pltpu.roll(x, 64, 1)
    return x + pltpu.roll(x, 32, 1)


def lane_group(rows):
    return lax.broadcasted_iota(jnp.int32, (rows, 128), 1) // 32


def pack(x, group):
    out = x[0:8]
    for g in range(1, 4):
        out = jnp.where(group == g, x[8 * g : 8 * g + 8], out)
    return out


def turn(x, groups):
    return x if groups % 4 == 0 else pltpu.roll(x, groups % 4 * 32, 1)


def kernel(
    policy_rows, action_rows, prev, costs, policy, targets, anchor, rel_out, q_out, gain_out,
    prev_buf, cost_buf, policy_buf, target_buf, anchor_buf, blocks, own_rows, actions, column, first_tile, acc, rest,
    cost_part, half_out, half_in, fresh, packed, gathered, combined, row_sums, message, arrived,
    in_sem, rows_sem, other_sem, act_sem, recv_sem, col_sem, half_sem, fresh_sem, q_sem,
    send_sem, psend_sem, csend_sem, hsend_sem, fsend_sem, qsend_sem,
):
    row, col = lax.axis_index("row"), lax.axis_index("col")
    core = row % 2
    z = row // 2 % 4
    y_lo = row // 8
    y_hi, x = col // 4, col % 4
    y = y_hi * 2 + y_lo

    def device(x, y, z, core):
        return ((y % 2 * 4 + z) * 2 + core, y // 2 * 4 + x)

    ways = [device((x + a) % 4, (y + b) % 4, (z + c) % 4, core) for a, b, c in HOPS]
    twin = (row + 1 - 2 * core, col)

    barrier = pltpu.get_barrier_semaphore()
    for other in ways + [twin]:
        pl.semaphore_signal(barrier, inc=1, device_id=other, device_id_type=MESH)

    load_prev = pltpu.make_async_copy(prev, prev_buf, in_sem.at[0])
    load_prev.start()

    def block_of(code, core):
        there = device((x - code // 16) % 4, (y - code // 4 % 4) % 4, (z - code % 4) % 4, core)
        return pl.multiple_of((there[0] * 8 + there[1]) * 1024, 1024)

    for n in range(64):
        pltpu.make_async_copy(
            policy_rows.at[:, pl.ds(block_of(ORDER[n], core), 1024)], own_rows.at[n, pl.ds(0, 32)], rows_sem.at[n // 4]
        ).start()

    small_loads = [
        pltpu.make_async_copy(source, target, in_sem.at[n + 1])
        for n, (source, target) in enumerate(
            ((costs, cost_buf), (policy, policy_buf), (targets, target_buf), (anchor, anchor_buf))
        )
    ]
    for copy in small_loads:
        copy.start()

    load_prev.wait()
    blocks[0] = prev_buf[...].astype(BF16)
    pl.semaphore_wait(barrier, 19)

    def wait_for(ref, sem):
        pltpu.make_async_copy(ref, ref, sem).wait()

    def send_rows():
        for n in range(64):
            pltpu.make_async_remote_copy(
                policy_rows.at[:, pl.ds(block_of(ORDER[n], 1 - core), 1024)], own_rows.at[n, pl.ds(32, 32)],
                psend_sem.at[0], other_sem.at[n // 4], device_id=twin, device_id_type=MESH,
            ).start()
        for n in range(CHUNKS):
            half, part = n % 2, n // 2
            pltpu.make_async_copy(
                action_rows.at[pl.ds(64 * part, 64), pl.ds(8 * half, 8)], actions.at[half, pl.ds(64 * part, 64)],
                act_sem.at[n],
            ).start()

    def part_cost():
        for copy in small_loads:
            copy.wait()
        chosen = policy_buf[...][:, None, :] == lax.broadcasted_iota(jnp.int32, (1, 8, 32), 1)
        cost = jnp.sum(jnp.where(chosen, cost_buf[...], 0.0), axis=1)
        cost_part[...] = jnp.concatenate([cost] * 4, axis=0).T

    def send_block(half, hop, source, target):
        pltpu.make_async_remote_copy(
            blocks.at[source, pl.ds(16 * half, 16)], blocks.at[target, pl.ds(16 * half, 16)],
            send_sem.at[0], recv_sem.at[half * 64 + target], device_id=ways[hop], device_id_type=MESH,
        ).start()

    slot = {code: n for n, code in enumerate(ORDER)}

    def forward_column():
        for n in range(8):
            y_other, z_other = n // 4, n % 4
            code = (y_lo - y_other + 4) % 4 * 4 + (z - z_other + 4) % 4
            where = 0
            for c in range(16):
                if c // 4 != 2:
                    where = where + jnp.where(code == c, slot[c], 0)
            place = n * 2 + core
            pltpu.make_async_remote_copy(
                blocks.at[where], column.at[place], csend_sem.at[0], col_sem.at[1], device_id=twin, device_id_type=MESH
            ).start()
            pltpu.make_async_copy(blocks.at[where], column.at[place], col_sem.at[0]).start()

    def policy_group(g):
        wait_for(own_rows.at[pl.ds(4 * g, 4), pl.ds(0, 32)], rows_sem.at[g])
        wait_for(own_rows.at[pl.ds(4 * g, 4), pl.ds(32, 32)], other_sem.at[g])
        left = own_rows[4 * g : 4 * g + 4].reshape(256, 1024)
        right = blocks[4 * g : 4 * g + 4].reshape(128, 1024)
        out = lax.dot_general(left, right, (((1,), (1,)), ((), ())), preferred_element_type=F32)
        acc[...] = out if g == 0 else acc[...] + out

    has_fresh = col < 4

    def action_chunk(n):
        half, part = n % 2, n // 2
        if n == 0:
            eight = column.at[pl.ds(0, 8)]
            wait_for(eight, col_sem.at[0])
            wait_for(eight, col_sem.at[1])
        here = pl.ds(64 * part, 64)
        wait_for(actions.at[half, here], act_sem.at[n])
        chunk = actions[half, here].reshape(512, 1024)
        values = column[8 * half : 8 * half + 8].reshape(256, 1024)
        out = lax.dot_general(chunk, values, (((1,), (1,)), ((), ())), preferred_element_type=F32)
        out = out.reshape(64, 8, 256)
        mine = lax.broadcasted_iota(jnp.int32, (8, 256), 0)
        theirs = lax.broadcasted_iota(jnp.int32, (8, 256), 1) // 32
        keep = mine == theirs
        if half == 0:
            keep = keep & ((theirs > 0) | jnp.logical_not(has_fresh))
        out = jnp.where(keep[None], out, 0.0)
        out = jnp.sum(out[:, :, 0:128] + out[:, :, 128:256], axis=1)
        if half == 0:
            rest[here] = out

            @pl.when(has_fresh)
            def _():
                pick = (
                    lax.broadcasted_iota(jnp.int32, (64, 512), 1) == 8 * lax.broadcasted_iota(jnp.int32, (64, 512), 0)
                ).astype(BF16)
                first_tile[here] = jnp.dot(pick, chunk, preferred_element_type=F32).astype(BF16)
        else:
            rest[here] = tile4(rest[here] + out)

    sent = 0
    for event in EVENTS:
        if event >= 1000:
            event, target = divmod(event - 1000, 64)
            event, source = divmod(event, 64)
            send_block(event % 2, event // 2, source, target)
            sent += 1
            if sent == 12:
                send_rows()
                part_cost()
        elif event >= 0:
            half, n = divmod(event, 64)
            wait_for(blocks.at[n, pl.ds(16 * half, 16)], recv_sem.at[event])
        elif event > -100:
            policy_group(-1 - event)
        elif event > -200:
            action_chunk(-101 - event)
        else:
            forward_column()

    group = lane_group(64)
    total = jnp.where(group == 0, acc[0:64, :], 0.0)
    for b in range(1, 4):
        total = jnp.where(group == b, acc[64 * b : 64 * b + 64, :], total)
    total = tile4(total)
    half_out[...] = total[32:64]
    swap = pltpu.make_async_remote_copy(
        half_out, half_in, hsend_sem.at[0], half_sem.at[0], device_id=twin, device_id_type=MESH
    )
    swap.start()
    mine = total[0:32] + cost_part[...]
    swap.wait_recv()
    mine = mine + half_in[...]
    fresh[...] = mine
    group = lane_group(32)
    small = lane_group(8)
    packed[...] = pack(mine, small)

    place = row % 4 * 8 + col
    target_col = row // 4
    is_target = col == target_col
    for k in range(1, 16):
        pltpu.make_async_remote_copy(
            packed, gathered.at[place], fsend_sem.at[0], fresh_sem.at[0],
            device_id=((row + k) % 16, target_col), device_id_type=MESH,
        ).start()

    @pl.when(is_target)
    def _():
        pltpu.make_async_copy(packed, gathered.at[place], fresh_sem.at[0]).start()

    @pl.when(jnp.logical_not(is_target))
    def _():
        pltpu.make_async_remote_copy(
            packed, gathered.at[place], fsend_sem.at[0], fresh_sem.at[0],
            device_id=(row, target_col), device_id_type=MESH,
        ).start()

    for n in range(CHUNKS_DURING, CHUNKS):
        action_chunk(n)

    @pl.when(has_fresh)
    def _():
        sums = lax.dot_general(
            jnp.ones((8, 1024), BF16), first_tile[...], (((1,), (1,)), ((), ())), preferred_element_type=F32
        )
        for c in range(8):
            row_sums[c] = turn(sums[:, 128 * (c // 4) : 128 * (c // 4) + 128], -c)

    @pl.when(has_fresh)
    def _():
        wait_for(gathered, fresh_sem.at[0])
        for n in range(32):
            line = gathered[n]
            high = line.astype(BF16).astype(F32)
            mid = (line - high).astype(BF16).astype(F32)
            low = line - high - mid
            for g in range(4):
                parts = jnp.where(
                    small == 0,
                    turn(high, -g),
                    jnp.where(small == 1, turn(mid, 1 - g), jnp.where(small == 2, turn(low, 2 - g), 0.0)),
                )
                combined[32 * n + 8 * g : 32 * n + 8 * g + 8] = parts.astype(BF16)
        states = col * 1024 + lax.broadcasted_iota(jnp.int32, (8, 1024), 1)
        chosen = (states == anchor_buf[...]).astype(BF16)
        gain = jnp.dot(chosen, combined[...], preferred_element_type=F32)
        late = jnp.dot(first_tile[...], combined[...], preferred_element_type=F32)
        values = rest[...] + tile4(late)
        first = lax.broadcasted_iota(jnp.int32, (8, 128), 0) == 0
        for c in range(8):
            message[c, 0:8] = pack(values[32 * c : 32 * c + 32], small)
            message[c, 8:16] = jnp.where(first, gain, row_sums[c])

    @pl.when(jnp.logical_not(has_fresh))
    def _():
        for c in range(8):
            message[c, 0:8] = pack(rest[32 * c : 32 * c + 32], small)
            message[c, 8:16] = jnp.zeros((8, 128), F32)

    for k in range(1, 8):
        other = (col + k) % 8
        pltpu.make_async_remote_copy(
            message.at[other], arrived.at[k - 1], qsend_sem.at[0], q_sem.at[0],
            device_id=(row, other), device_id_type=MESH,
        ).start()
    total = message[col]
    wait_for(arrived, q_sem.at[0])
    for k in range(7):
        total = total + arrived[k]
    gain = tile4(total[8:16])[0:1]
    values = jnp.concatenate([turn(total[0:8], 1 - g) for g in range(4)], axis=0)
    both = jnp.where(group == 0, fresh[...], jnp.where(group == 1, values, gain)).T
    rel_out[...] = both[0:32]
    gain_out[...] = both[64:96]
    q_out[...] = both[32:64] - both[64:96] * total[9:10, 0:32] + target_buf[...]

    wait_for(blocks.at[pl.ds(0, 63)], send_sem.at[0])
    wait_for(own_rows.at[:, pl.ds(32, 32)], psend_sem.at[0])
    wait_for(column.at[pl.ds(0, 8)], csend_sem.at[0])
    swap.wait_send()

    @pl.when(is_target)
    def _():
        wait_for(gathered.at[pl.ds(0, 15)], fsend_sem.at[0])

    @pl.when(jnp.logical_not(is_target))
    def _():
        wait_for(gathered.at[pl.ds(0, 16)], fsend_sem.at[0])

    wait_for(arrived, qsend_sem.at[0])


def local(policy_rows, action_rows, prev_values, action_costs, policy, target_costs, anchor):
    any_spec = pl.BlockSpec(memory_space=pl.ANY)
    dma = pltpu.SemaphoreType.DMA
    fresh, values, gain = pl.pallas_call(
        kernel,
        out_shape=[jax.ShapeDtypeStruct((32, 32), F32)] * 3,
        in_specs=[any_spec] * 7,
        out_specs=[pl.BlockSpec(memory_space=pltpu.VMEM)] * 3,
        scratch_shapes=[
            pltpu.VMEM((32, 1024), F32),
            pltpu.VMEM((32, 8, 32), F32),
            pltpu.VMEM((1, 32), jnp.int32),
            pltpu.VMEM((32, 32), F32),
            pltpu.VMEM((1, 1), jnp.int32),
            pltpu.VMEM((64, 32, 1024), BF16),
            pltpu.VMEM((64, 64, 1024), BF16),
            pltpu.VMEM((2, 256, 8, 1024), BF16),
            pltpu.VMEM((16, 32, 1024), BF16),
            pltpu.VMEM((256, 1024), BF16),
            pltpu.VMEM((256, 128), F32),
            pltpu.VMEM((256, 128), F32),
            pltpu.VMEM((32, 128), F32),
            pltpu.VMEM((32, 128), F32),
            pltpu.VMEM((32, 128), F32),
            pltpu.VMEM((32, 128), F32),
            pltpu.VMEM((8, 128), F32),
            pltpu.VMEM((32, 8, 128), F32),
            pltpu.VMEM((1024, 128), BF16),
            pltpu.VMEM((8, 8, 128), F32),
            pltpu.VMEM((8, 16, 128), F32),
            pltpu.VMEM((7, 16, 128), F32),
            dma((5,)), dma((16,)), dma((16,)), dma((8,)), dma((128,)), dma((2,)), dma((1,)), dma((1,)), dma((1,)),
            dma((1,)), dma((1,)), dma((1,)), dma((1,)), dma((1,)), dma((1,)),
        ],
        compiler_params=pltpu.CompilerParams(
            collective_id=0, has_side_effects=True, vmem_limit_bytes=60 * 1024 * 1024
        ),
    )(
        policy_rows,
        action_rows.reshape(action_rows.shape[0], 16, 1024),
        prev_values,
        action_costs,
        policy.reshape(1, 32),
        target_costs,
        anchor.reshape(1, 1),
    )
    return fresh - gain, values - gain


def solution(mesh):
    in_specs = (
        P(("row", "col"), None),
        P("row", None, "col", None),
        P(None, ("row", "col")),
        P(None, None, ("row", "col")),
        P(("row", "col")),
        P(None, ("row", "col")),
        P(),
    )
    out_specs = (P(None, ("row", "col")), P(None, ("row", "col")))
    return jax.shard_map(local, mesh=mesh, in_specs=in_specs, out_specs=out_specs, check_vma=False)
```

```python
import functools

import jax
import jax.numpy as jnp
from jax import lax
from jax.experimental import pallas as pl
from jax.experimental.pallas import tpu as pltpu
from jax.sharding import PartitionSpec as P

MESH = pl.DeviceIdType.MESH
F32, BF16 = jnp.float32, jnp.bfloat16
STEPS = ((1, 0, 0), (3, 0, 0), (0, 1, 0), (0, 3, 0), (0, 0, 1), (0, 0, 3))
ORDER = (
    0, 1, 3, 4, 12, 16, 48, 15, 60, 5, 13, 2, 7, 8, 20, 51, 28, 19, 49, 52, 6, 14, 63, 29, 35, 55, 9, 36, 44, 53, 50,
    61, 18, 24, 11, 10, 22, 30, 45, 47, 54, 57, 40, 34, 62, 37, 23, 39, 59, 25, 32, 21, 17, 27, 43, 26, 33, 46, 58, 56,
    31, 38, 41, 42,
)
EVENTS = (
    5101, 9198, 17387, 25580, 33769, 46058, 1005, 13294, 21483, 29676, 37865, 41962, 54262, 107511, 136178, 95216,
    70684, 123892, 1, 9274, 4, 1272, 17457, 66, 29807, 33843, 42223, 9456, 5241, 25650, 65, 21553, 2, 3, 67, -1, 37939,
    46260, 70, 13722, 1206, 17589, 68, 29941, 46455, 69, 30008, 74, 38525, 15, 10176, 5759, 18369, 38266, 5, 42297,
    13499, 78, 6019, 6, 17787, 30338, 72, 46590, 22409, 18, 10400, 9, 34364, 1627, 71, 30154, 7, 42429, 11, 1736, 18565,
    26558, -2, 8, 9732, 73, 38460, 16, 34815, 76, 14081, 17986, 10, 75, -3, 114, 49280, 32900, 14, 1923, 38407, 79,
    47046, 13893, 12, 13, 77, -4, 24, 18967, 87, 6606, 31193, 39373, 42950, 9863, 5832, 26633, 91, 23250, 80, 17, 81,
    82, 19, 83, -5, 39637, 86, 14735, 1508, 20, 18699, 26058, 97, 48221, 46998, 84, 21, 85, -201, 10083, 6412, 31051,
    29, 35664, 32, 19468, 43539, 23, 35277, 98, 15512, 2510, 19281, 27151, 22, -6, 88, 25, 89, 26, 90, 27, -7, 43412,
    14993, 28, 27410, 93, 39760, 113, 8294, 47, 20446, 95, 39892, 47635, 11093, 1814, 23063, 27032, 92, 30, 94, 31, -8,
    -101, 33, 35929, 56, 45594, 109, 16219, 101, 7521, 18908, 60, 29469, 41055, 106, 48798, 40, 11813, 35, 3295, 20002,
    32608, 96, 34, 99, -9, -102, 14179, 100, 7461, 117, 24932, 112, 49186, 38, 36257, 28070, 36, 37, 102, 39, 103, -10,
    126, 41895, 54, 45479, -103, 104, 41, 105, 42, 43, 107, -11, 44, 108, 45, 46, 110, 111, -12, 48, 49, 50, 51, 115,
    -13, -104, 52, 116, 53, 118, 55, 119, -14, 120, 57, 121, 58, 122, 59, 123, -15, 124, 61, 125, 62, 63, 127, -16,
)
CHUNKS_DURING = 4
CHUNKS = 8


def hops_of():
    hops = [STEPS[i] for i in range(6)]
    for a in range(6):
        for b in range(a + 1, 6):
            if a // 2 != b // 2:
                hops.append(tuple((p + q) % 4 for p, q in zip(STEPS[a], STEPS[b])))
    return hops


HOPS = hops_of()


def tile4(x):
    x = x + pltpu.roll(x, 64, 1)
    return x + pltpu.roll(x, 32, 1)


def lane_group(rows):
    return lax.broadcasted_iota(jnp.int32, (rows, 128), 1) // 32


def pack(x, group):
    out = x[0:8]
    for g in range(1, 4):
        out = jnp.where(group == g, x[8 * g : 8 * g + 8], out)
    return out


def turn(x, groups):
    return x if groups % 4 == 0 else pltpu.roll(x, groups % 4 * 32, 1)


def kernel(
    policy_rows, action_rows, prev, costs, policy, targets, anchor, out,
    prev_buf, cost_buf, policy_buf, target_buf, anchor_buf, blocks, own_rows, actions, column, first_tile, acc, rest,
    cost_part, half_out, half_in, fresh, packed, gathered, combined, row_sums, message, arrived,
    in_sem, rows_sem, other_sem, act_sem, recv_sem, col_sem, half_sem, fresh_sem, q_sem,
    send_sem, psend_sem, csend_sem, hsend_sem, fsend_sem, qsend_sem,
):
    row, col = lax.axis_index("row"), lax.axis_index("col")
    core = row % 2
    z = row // 2 % 4
    y_lo = row // 8
    y_hi, x = col // 4, col % 4
    y = y_hi * 2 + y_lo

    def device(x, y, z, core):
        return ((y % 2 * 4 + z) * 2 + core, y // 2 * 4 + x)

    ways = [device((x + a) % 4, (y + b) % 4, (z + c) % 4, core) for a, b, c in HOPS]
    twin = (row + 1 - 2 * core, col)

    barrier = pltpu.get_barrier_semaphore()
    for other in ways + [twin]:
        pl.semaphore_signal(barrier, inc=1, device_id=other, device_id_type=MESH)

    load_prev = pltpu.make_async_copy(prev, prev_buf, in_sem.at[0])
    load_prev.start()

    def block_of(code, core):
        there = device((x - code // 16) % 4, (y - code // 4 % 4) % 4, (z - code % 4) % 4, core)
        return pl.multiple_of((there[0] * 8 + there[1]) * 1024, 1024)

    for n in range(64):
        pltpu.make_async_copy(
            policy_rows.at[:, pl.ds(block_of(ORDER[n], core), 1024)], own_rows.at[n, pl.ds(0, 32)], rows_sem.at[n // 4]
        ).start()

    small_loads = [
        pltpu.make_async_copy(source, target, in_sem.at[n + 1])
        for n, (source, target) in enumerate(
            ((costs, cost_buf), (policy, policy_buf), (targets, target_buf), (anchor, anchor_buf))
        )
    ]
    for copy in small_loads:
        copy.start()

    load_prev.wait()
    blocks[0] = prev_buf[...].astype(BF16)
    pl.semaphore_wait(barrier, 19)

    def wait_for(ref, sem):
        pltpu.make_async_copy(ref, ref, sem).wait()

    def send_rows():
        for n in range(64):
            pltpu.make_async_remote_copy(
                policy_rows.at[:, pl.ds(block_of(ORDER[n], 1 - core), 1024)], own_rows.at[n, pl.ds(32, 32)],
                psend_sem.at[0], other_sem.at[n // 4], device_id=twin, device_id_type=MESH,
            ).start()
        for n in range(CHUNKS):
            half, part = n % 2, n // 2
            pltpu.make_async_copy(
                action_rows.at[pl.ds(64 * part, 64), pl.ds(8 * half, 8)], actions.at[half, pl.ds(64 * part, 64)],
                act_sem.at[n],
            ).start()

    def part_cost():
        for copy in small_loads:
            copy.wait()
        chosen = policy_buf[...][:, None, :] == lax.broadcasted_iota(jnp.int32, (1, 8, 32), 1)
        cost = jnp.sum(jnp.where(chosen, cost_buf[...], 0.0), axis=1)
        cost_part[...] = jnp.concatenate([cost] * 4, axis=0).T

    def send_block(half, hop, source, target):
        pltpu.make_async_remote_copy(
            blocks.at[source, pl.ds(16 * half, 16)], blocks.at[target, pl.ds(16 * half, 16)],
            send_sem.at[0], recv_sem.at[half * 64 + target], device_id=ways[hop], device_id_type=MESH,
        ).start()

    slot = {code: n for n, code in enumerate(ORDER)}

    def forward_column():
        for n in range(8):
            y_other, z_other = n // 4, n % 4
            code = (y_lo - y_other + 4) % 4 * 4 + (z - z_other + 4) % 4
            where = 0
            for c in range(16):
                if c // 4 != 2:
                    where = where + jnp.where(code == c, slot[c], 0)
            place = n * 2 + core
            pltpu.make_async_remote_copy(
                blocks.at[where], column.at[place], csend_sem.at[0], col_sem.at[1], device_id=twin, device_id_type=MESH
            ).start()
            pltpu.make_async_copy(blocks.at[where], column.at[place], col_sem.at[0]).start()

    def policy_group(g):
        wait_for(own_rows.at[pl.ds(4 * g, 4), pl.ds(0, 32)], rows_sem.at[g])
        wait_for(own_rows.at[pl.ds(4 * g, 4), pl.ds(32, 32)], other_sem.at[g])
        left = own_rows[4 * g : 4 * g + 4].reshape(256, 1024)
        right = blocks[4 * g : 4 * g + 4].reshape(128, 1024)
        product = lax.dot_general(left, right, (((1,), (1,)), ((), ())), preferred_element_type=F32)
        acc[...] = product if g == 0 else acc[...] + product

    has_fresh = col < 4

    def action_chunk(n):
        half, part = n % 2, n // 2
        if n == 0:
            eight = column.at[pl.ds(0, 8)]
            wait_for(eight, col_sem.at[0])
            wait_for(eight, col_sem.at[1])
        here = pl.ds(64 * part, 64)
        wait_for(actions.at[half, here], act_sem.at[n])
        chunk = actions[half, here].reshape(512, 1024)
        values = column[8 * half : 8 * half + 8].reshape(256, 1024)
        product = lax.dot_general(chunk, values, (((1,), (1,)), ((), ())), preferred_element_type=F32)
        product = product.reshape(64, 8, 256)
        mine = lax.broadcasted_iota(jnp.int32, (8, 256), 0)
        theirs = lax.broadcasted_iota(jnp.int32, (8, 256), 1) // 32
        keep = mine == theirs
        if half == 0:
            keep = keep & ((theirs > 0) | jnp.logical_not(has_fresh))
        product = jnp.where(keep[None], product, 0.0)
        product = jnp.sum(product[:, :, 0:128] + product[:, :, 128:256], axis=1)
        if half == 0:
            rest[here] = product

            @pl.when(has_fresh)
            def _():
                pick = (
                    lax.broadcasted_iota(jnp.int32, (64, 512), 1) == 8 * lax.broadcasted_iota(jnp.int32, (64, 512), 0)
                ).astype(BF16)
                first_tile[here] = jnp.dot(pick, chunk, preferred_element_type=F32).astype(BF16)
        else:
            rest[here] = tile4(rest[here] + product)

    sent = 0
    for event in EVENTS:
        if event >= 1000:
            event, target = divmod(event - 1000, 64)
            event, source = divmod(event, 64)
            send_block(event % 2, event // 2, source, target)
            sent += 1
            if sent == 12:
                send_rows()
                part_cost()
        elif event >= 0:
            half, n = divmod(event, 64)
            wait_for(blocks.at[n, pl.ds(16 * half, 16)], recv_sem.at[event])
        elif event > -100:
            policy_group(-1 - event)
        elif event > -200:
            action_chunk(-101 - event)
        else:
            forward_column()

    group = lane_group(64)
    total = jnp.where(group == 0, acc[0:64, :], 0.0)
    for b in range(1, 4):
        total = jnp.where(group == b, acc[64 * b : 64 * b + 64, :], total)
    total = tile4(total)
    half_out[...] = total[32:64]
    swap = pltpu.make_async_remote_copy(
        half_out, half_in, hsend_sem.at[0], half_sem.at[0], device_id=twin, device_id_type=MESH
    )
    swap.start()
    mine = total[0:32] + cost_part[...]
    swap.wait_recv()
    mine = mine + half_in[...]
    fresh[...] = mine
    group = lane_group(32)
    small = lane_group(8)
    packed[...] = pack(mine, small)

    place = row % 4 * 8 + col
    target_col = row // 4
    is_target = col == target_col
    for k in range(1, 16):
        pltpu.make_async_remote_copy(
            packed, gathered.at[place], fsend_sem.at[0], fresh_sem.at[0],
            device_id=((row + k) % 16, target_col), device_id_type=MESH,
        ).start()

    @pl.when(is_target)
    def _():
        pltpu.make_async_copy(packed, gathered.at[place], fresh_sem.at[0]).start()

    @pl.when(jnp.logical_not(is_target))
    def _():
        pltpu.make_async_remote_copy(
            packed, gathered.at[place], fsend_sem.at[0], fresh_sem.at[0],
            device_id=(row, target_col), device_id_type=MESH,
        ).start()

    for n in range(CHUNKS_DURING, CHUNKS):
        action_chunk(n)

    @pl.when(has_fresh)
    def _():
        sums = lax.dot_general(
            jnp.ones((8, 1024), BF16), first_tile[...], (((1,), (1,)), ((), ())), preferred_element_type=F32
        )
        for c in range(8):
            row_sums[c] = turn(sums[:, 128 * (c // 4) : 128 * (c // 4) + 128], -c)

    @pl.when(has_fresh)
    def _():
        wait_for(gathered, fresh_sem.at[0])
        for n in range(32):
            line = gathered[n]
            high = line.astype(BF16).astype(F32)
            mid = (line - high).astype(BF16).astype(F32)
            low = line - high - mid
            for g in range(4):
                parts = jnp.where(
                    small == 0,
                    turn(high, -g),
                    jnp.where(small == 1, turn(mid, 1 - g), jnp.where(small == 2, turn(low, 2 - g), 0.0)),
                )
                combined[32 * n + 8 * g : 32 * n + 8 * g + 8] = parts.astype(BF16)
        states = col * 1024 + lax.broadcasted_iota(jnp.int32, (8, 1024), 1)
        chosen = (states == anchor_buf[...]).astype(BF16)
        gain = jnp.dot(chosen, combined[...], preferred_element_type=F32)
        late = jnp.dot(first_tile[...], combined[...], preferred_element_type=F32)
        values = rest[...] + tile4(late)
        first = lax.broadcasted_iota(jnp.int32, (8, 128), 0) == 0
        for c in range(8):
            message[c, 0:8] = pack(values[32 * c : 32 * c + 32], small)
            message[c, 8:16] = jnp.where(first, gain, row_sums[c])

    @pl.when(jnp.logical_not(has_fresh))
    def _():
        for c in range(8):
            message[c, 0:8] = pack(rest[32 * c : 32 * c + 32], small)
            message[c, 8:16] = jnp.zeros((8, 128), F32)

    for k in range(1, 8):
        other = (col + k) % 8
        pltpu.make_async_remote_copy(
            message.at[other], arrived.at[k - 1], qsend_sem.at[0], q_sem.at[0],
            device_id=(row, other), device_id_type=MESH,
        ).start()
    total = message[col]
    wait_for(arrived, q_sem.at[0])
    for k in range(7):
        total = total + arrived[k]
    gain = tile4(total[8:16])[0:1]
    values = jnp.concatenate([turn(total[0:8], 1 - g) for g in range(4)], axis=0)
    both = jnp.where(group == 0, fresh[...], jnp.where(group == 1, values, gain)).T
    out[0:32] = both[0:32]
    out[64:96] = both[64:96]
    out[32:64] = both[32:64] - both[64:96] * total[9:10, 0:32] + target_buf[...]

    wait_for(blocks.at[pl.ds(0, 63)], send_sem.at[0])
    wait_for(own_rows.at[:, pl.ds(32, 32)], psend_sem.at[0])
    wait_for(column.at[pl.ds(0, 8)], csend_sem.at[0])
    swap.wait_send()

    @pl.when(is_target)
    def _():
        wait_for(gathered.at[pl.ds(0, 15)], fsend_sem.at[0])

    @pl.when(jnp.logical_not(is_target))
    def _():
        wait_for(gathered.at[pl.ds(0, 16)], fsend_sem.at[0])

    wait_for(arrived, qsend_sem.at[0])


def local(policy_rows, action_rows, prev_values, action_costs, policy, target_costs, anchor):
    any_spec = pl.BlockSpec(memory_space=pl.ANY)
    dma = pltpu.SemaphoreType.DMA
    out = pl.pallas_call(
        kernel,
        out_shape=jax.ShapeDtypeStruct((96, 32), F32),
        in_specs=[any_spec] * 7,
        out_specs=pl.BlockSpec(memory_space=pltpu.VMEM),
        scratch_shapes=[
            pltpu.VMEM((32, 1024), F32),
            pltpu.VMEM((32, 8, 32), F32),
            pltpu.VMEM((1, 32), jnp.int32),
            pltpu.VMEM((32, 32), F32),
            pltpu.VMEM((1, 1), jnp.int32),
            pltpu.VMEM((64, 32, 1024), BF16),
            pltpu.VMEM((64, 64, 1024), BF16),
            pltpu.VMEM((2, 256, 8, 1024), BF16),
            pltpu.VMEM((16, 32, 1024), BF16),
            pltpu.VMEM((256, 1024), BF16),
            pltpu.VMEM((256, 128), F32),
            pltpu.VMEM((256, 128), F32),
            pltpu.VMEM((32, 128), F32),
            pltpu.VMEM((32, 128), F32),
            pltpu.VMEM((32, 128), F32),
            pltpu.VMEM((32, 128), F32),
            pltpu.VMEM((8, 128), F32),
            pltpu.VMEM((32, 8, 128), F32),
            pltpu.VMEM((1024, 128), BF16),
            pltpu.VMEM((8, 8, 128), F32),
            pltpu.VMEM((8, 16, 128), F32),
            pltpu.VMEM((7, 16, 128), F32),
            dma((5,)), dma((16,)), dma((16,)), dma((8,)), dma((128,)), dma((2,)), dma((1,)), dma((1,)), dma((1,)),
            dma((1,)), dma((1,)), dma((1,)), dma((1,)), dma((1,)), dma((1,)),
        ],
        compiler_params=pltpu.CompilerParams(
            collective_id=0, has_side_effects=True, vmem_limit_bytes=60 * 1024 * 1024
        ),
    )(
        policy_rows,
        action_rows.reshape(action_rows.shape[0], 16, 1024),
        prev_values,
        action_costs,
        policy.reshape(1, 32),
        target_costs,
        anchor.reshape(1, 1),
    )
    return out[0:32] - out[64:96], out[32:64] - out[64:96]


def solution(mesh):
    in_specs = (
        P(("row", "col"), None),
        P("row", None, "col", None),
        P(None, ("row", "col")),
        P(None, None, ("row", "col")),
        P(("row", "col")),
        P(None, ("row", "col")),
        P(),
    )
    out_specs = (P(None, ("row", "col")), P(None, ("row", "col")))
    return jax.shard_map(local, mesh=mesh, in_specs=in_specs, out_specs=out_specs, check_vma=False)
```

```python
import functools

import jax
import jax.numpy as jnp
from jax import lax
from jax.experimental import pallas as pl
from jax.experimental.pallas import tpu as pltpu
from jax.sharding import PartitionSpec as P

MESH = pl.DeviceIdType.MESH
F32, BF16 = jnp.float32, jnp.bfloat16
STEPS = ((1, 0, 0), (3, 0, 0), (0, 1, 0), (0, 3, 0), (0, 0, 1), (0, 0, 3))
ORDER = (
    0, 1, 3, 4, 12, 16, 48, 15, 60, 5, 13, 2, 7, 8, 20, 51, 28, 19, 49, 52, 6, 14, 63, 29, 35, 55, 9, 36, 44, 53, 50,
    61, 18, 24, 11, 10, 22, 30, 45, 47, 54, 57, 40, 34, 62, 37, 23, 39, 59, 25, 32, 21, 17, 27, 43, 26, 33, 46, 58, 56,
    31, 38, 41, 42,
)
EVENTS = (
    5101, 9198, 17387, 25580, 33769, 46058, 1005, 13294, 21483, 29676, 37865, 41962, 54262, 107511, 136178, 95216,
    70684, 123892, 1, 9274, 4, 1272, 17457, 66, 29807, 33843, 42223, 9456, 5241, 25650, 65, 21553, 2, 3, 67, -1, 37939,
    46260, 70, 13722, 1206, 17589, 68, 29941, 46455, 69, 30008, 74, 38525, 15, 10176, 5759, 18369, 38266, 5, 42297,
    13499, 78, 6019, 6, 17787, 30338, 72, 46590, 22409, 18, 10400, 9, 34364, 1627, 71, 30154, 7, 42429, 11, 1736, 18565,
    26558, -2, 8, 9732, 73, 38460, 16, 34815, 76, 14081, 17986, 10, 75, -3, 114, 49280, 32900, 14, 1923, 38407, 79,
    47046, 13893, 12, 13, 77, -4, 24, 18967, 87, 6606, 31193, 39373, 42950, 9863, 5832, 26633, 91, 23250, 80, 17, 81,
    82, 19, 83, -5, 39637, 86, 14735, 1508, 20, 18699, 26058, 97, 48221, 46998, 84, 21, 85, -201, 10083, 6412, 31051,
    29, 35664, 32, 19468, 43539, 23, 35277, 98, 15512, 2510, 19281, 27151, 22, -6, 88, 25, 89, 26, 90, 27, -7, 43412,
    14993, 28, 27410, 93, 39760, 113, 8294, 47, 20446, 95, 39892, 47635, 11093, 1814, 23063, 27032, 92, 30, 94, 31, -8,
    -101, 33, 35929, 56, 45594, 109, 16219, 101, 7521, 18908, 60, 29469, 41055, 106, 48798, 40, 11813, 35, 3295, 20002,
    32608, 96, 34, 99, -9, -102, 14179, 100, 7461, 117, 24932, 112, 49186, 38, 36257, 28070, 36, 37, 102, 39, 103, -10,
    126, 41895, 54, 45479, -103, 104, 41, 105, 42, 43, 107, -11, 44, 108, 45, 46, 110, 111, -12, 48, 49, 50, 51, 115,
    -13, -104, 52, 116, 53, 118, 55, 119, -14, 120, 57, 121, 58, 122, 59, 123, -15, 124, 61, 125, 62, 63, 127, -16,
)
CHUNKS_DURING = 4
CHUNKS = 8


def hops_of():
    hops = [STEPS[i] for i in range(6)]
    for a in range(6):
        for b in range(a + 1, 6):
            if a // 2 != b // 2:
                hops.append(tuple((p + q) % 4 for p, q in zip(STEPS[a], STEPS[b])))
    return hops


HOPS = hops_of()


def tile4(x):
    x = x + pltpu.roll(x, 64, 1)
    return x + pltpu.roll(x, 32, 1)


def lane_group(rows):
    return lax.broadcasted_iota(jnp.int32, (rows, 128), 1) // 32


def pack(x, group):
    out = x[0:8]
    for g in range(1, 4):
        out = jnp.where(group == g, x[8 * g : 8 * g + 8], out)
    return out


def turn(x, groups):
    return x if groups % 4 == 0 else pltpu.roll(x, groups % 4 * 32, 1)


def kernel(
    policy_rows, action_rows, prev, costs, policy, targets, anchor, out,
    prev_buf, cost_buf, policy_buf, target_buf, anchor_buf, blocks, own_rows, actions, column, first_tile, acc, rest,
    cost_part, half_out, half_in, fresh, packed, gathered, combined, row_sums, message, arrived,
    in_sem, rows_sem, other_sem, act_sem, recv_sem, col_sem, half_sem, fresh_sem, q_sem,
    send_sem, psend_sem, csend_sem, hsend_sem, fsend_sem, qsend_sem,
):
    row, col = lax.axis_index("row"), lax.axis_index("col")
    core = row % 2
    z = row // 2 % 4
    y_lo = row // 8
    y_hi, x = col // 4, col % 4
    y = y_hi * 2 + y_lo

    def device(x, y, z, core):
        return ((y % 2 * 4 + z) * 2 + core, y // 2 * 4 + x)

    ways = [device((x + a) % 4, (y + b) % 4, (z + c) % 4, core) for a, b, c in HOPS]
    twin = (row + 1 - 2 * core, col)

    barrier = pltpu.get_barrier_semaphore()
    used = sorted({(event - 1000) // 8192 for event in EVENTS if event >= 1000})
    senders = [device((x - a) % 4, (y - b) % 4, (z - c) % 4, core) for a, b, c in (HOPS[i] for i in used)]
    for other in senders + [twin]:
        pl.semaphore_signal(barrier, inc=1, device_id=other, device_id_type=MESH)

    load_prev = pltpu.make_async_copy(prev, prev_buf, in_sem.at[0])
    load_prev.start()

    def block_of(code, core):
        there = device((x - code // 16) % 4, (y - code // 4 % 4) % 4, (z - code % 4) % 4, core)
        return pl.multiple_of((there[0] * 8 + there[1]) * 1024, 1024)

    for n in range(64):
        pltpu.make_async_copy(
            policy_rows.at[:, pl.ds(block_of(ORDER[n], core), 1024)], own_rows.at[n, pl.ds(0, 32)], rows_sem.at[n // 4]
        ).start()

    small_loads = [
        pltpu.make_async_copy(source, target, in_sem.at[n + 1])
        for n, (source, target) in enumerate(
            ((costs, cost_buf), (policy, policy_buf), (targets, target_buf), (anchor, anchor_buf))
        )
    ]
    for copy in small_loads:
        copy.start()

    load_prev.wait()
    blocks[0] = prev_buf[...].astype(BF16)
    pl.semaphore_wait(barrier, len(senders) + 1)

    def wait_for(ref, sem):
        pltpu.make_async_copy(ref, ref, sem).wait()

    def send_rows():
        for n in range(64):
            pltpu.make_async_remote_copy(
                policy_rows.at[:, pl.ds(block_of(ORDER[n], 1 - core), 1024)], own_rows.at[n, pl.ds(32, 32)],
                psend_sem.at[0], other_sem.at[n // 4], device_id=twin, device_id_type=MESH,
            ).start()
        for n in range(CHUNKS):
            half, part = n % 2, n // 2
            pltpu.make_async_copy(
                action_rows.at[pl.ds(64 * part, 64), pl.ds(8 * half, 8)], actions.at[half, pl.ds(64 * part, 64)],
                act_sem.at[n],
            ).start()

    def part_cost():
        for copy in small_loads:
            copy.wait()
        chosen = policy_buf[...][:, None, :] == lax.broadcasted_iota(jnp.int32, (1, 8, 32), 1)
        cost = jnp.sum(jnp.where(chosen, cost_buf[...], 0.0), axis=1)
        cost_part[...] = jnp.concatenate([cost] * 4, axis=0).T

    def send_block(half, hop, source, target):
        pltpu.make_async_remote_copy(
            blocks.at[source, pl.ds(16 * half, 16)], blocks.at[target, pl.ds(16 * half, 16)],
            send_sem.at[0], recv_sem.at[half * 64 + target], device_id=ways[hop], device_id_type=MESH,
        ).start()

    slot = {code: n for n, code in enumerate(ORDER)}

    def forward_column():
        for n in range(8):
            y_other, z_other = n // 4, n % 4
            code = (y_lo - y_other + 4) % 4 * 4 + (z - z_other + 4) % 4
            where = 0
            for c in range(16):
                if c // 4 != 2:
                    where = where + jnp.where(code == c, slot[c], 0)
            place = n * 2 + core
            pltpu.make_async_remote_copy(
                blocks.at[where], column.at[place], csend_sem.at[0], col_sem.at[1], device_id=twin, device_id_type=MESH
            ).start()
            pltpu.make_async_copy(blocks.at[where], column.at[place], col_sem.at[0]).start()

    def policy_group(g):
        wait_for(own_rows.at[pl.ds(4 * g, 4), pl.ds(0, 32)], rows_sem.at[g])
        wait_for(own_rows.at[pl.ds(4 * g, 4), pl.ds(32, 32)], other_sem.at[g])
        left = own_rows[4 * g : 4 * g + 4].reshape(256, 1024)
        right = blocks[4 * g : 4 * g + 4].reshape(128, 1024)
        product = lax.dot_general(left, right, (((1,), (1,)), ((), ())), preferred_element_type=F32)
        acc[...] = product if g == 0 else acc[...] + product

    has_fresh = col < 4

    def action_chunk(n):
        half, part = n % 2, n // 2
        if n == 0:
            eight = column.at[pl.ds(0, 8)]
            wait_for(eight, col_sem.at[0])
            wait_for(eight, col_sem.at[1])
        here = pl.ds(64 * part, 64)
        wait_for(actions.at[half, here], act_sem.at[n])
        chunk = actions[half, here].reshape(512, 1024)
        values = column[8 * half : 8 * half + 8].reshape(256, 1024)
        product = lax.dot_general(chunk, values, (((1,), (1,)), ((), ())), preferred_element_type=F32)
        product = product.reshape(64, 8, 256)
        mine = lax.broadcasted_iota(jnp.int32, (8, 256), 0)
        theirs = lax.broadcasted_iota(jnp.int32, (8, 256), 1) // 32
        keep = mine == theirs
        if half == 0:
            keep = keep & ((theirs > 0) | jnp.logical_not(has_fresh))
        product = jnp.where(keep[None], product, 0.0)
        product = jnp.sum(product[:, :, 0:128] + product[:, :, 128:256], axis=1)
        if half == 0:
            rest[here] = product

            @pl.when(has_fresh)
            def _():
                pick = (
                    lax.broadcasted_iota(jnp.int32, (64, 512), 1) == 8 * lax.broadcasted_iota(jnp.int32, (64, 512), 0)
                ).astype(BF16)
                first_tile[here] = jnp.dot(pick, chunk, preferred_element_type=F32).astype(BF16)
        else:
            rest[here] = tile4(rest[here] + product)

    sent = 0
    for event in EVENTS:
        if event >= 1000:
            event, target = divmod(event - 1000, 64)
            event, source = divmod(event, 64)
            send_block(event % 2, event // 2, source, target)
            sent += 1
            if sent == 12:
                send_rows()
                part_cost()
        elif event >= 0:
            half, n = divmod(event, 64)
            wait_for(blocks.at[n, pl.ds(16 * half, 16)], recv_sem.at[event])
        elif event > -100:
            policy_group(-1 - event)
        elif event > -200:
            action_chunk(-101 - event)
        else:
            forward_column()

    group = lane_group(64)
    total = jnp.where(group == 0, acc[0:64, :], 0.0)
    for b in range(1, 4):
        total = jnp.where(group == b, acc[64 * b : 64 * b + 64, :], total)
    total = tile4(total)
    half_out[...] = total[32:64]
    swap = pltpu.make_async_remote_copy(
        half_out, half_in, hsend_sem.at[0], half_sem.at[0], device_id=twin, device_id_type=MESH
    )
    swap.start()
    mine = total[0:32] + cost_part[...]
    swap.wait_recv()
    mine = mine + half_in[...]
    fresh[...] = mine
    group = lane_group(32)
    small = lane_group(8)
    packed[...] = pack(mine, small)

    place = row % 4 * 8 + col
    target_col = row // 4
    is_target = col == target_col
    for k in range(1, 16):
        pltpu.make_async_remote_copy(
            packed, gathered.at[place], fsend_sem.at[0], fresh_sem.at[0],
            device_id=((row + k) % 16, target_col), device_id_type=MESH,
        ).start()

    @pl.when(is_target)
    def _():
        pltpu.make_async_copy(packed, gathered.at[place], fresh_sem.at[0]).start()

    @pl.when(jnp.logical_not(is_target))
    def _():
        pltpu.make_async_remote_copy(
            packed, gathered.at[place], fsend_sem.at[0], fresh_sem.at[0],
            device_id=(row, target_col), device_id_type=MESH,
        ).start()

    for n in range(CHUNKS_DURING, CHUNKS):
        action_chunk(n)

    @pl.when(has_fresh)
    def _():
        sums = lax.dot_general(
            jnp.ones((8, 1024), BF16), first_tile[...], (((1,), (1,)), ((), ())), preferred_element_type=F32
        )
        for c in range(8):
            row_sums[c] = turn(sums[:, 128 * (c // 4) : 128 * (c // 4) + 128], -c)

    @pl.when(has_fresh)
    def _():
        wait_for(gathered, fresh_sem.at[0])
        for n in range(32):
            line = gathered[n]
            high = line.astype(BF16).astype(F32)
            mid = (line - high).astype(BF16).astype(F32)
            low = line - high - mid
            for g in range(4):
                parts = jnp.where(
                    small == 0,
                    turn(high, -g),
                    jnp.where(small == 1, turn(mid, 1 - g), jnp.where(small == 2, turn(low, 2 - g), 0.0)),
                )
                combined[32 * n + 8 * g : 32 * n + 8 * g + 8] = parts.astype(BF16)
        states = col * 1024 + lax.broadcasted_iota(jnp.int32, (8, 1024), 1)
        chosen = (states == anchor_buf[...]).astype(BF16)
        gain = jnp.dot(chosen, combined[...], preferred_element_type=F32)
        late = jnp.dot(first_tile[...], combined[...], preferred_element_type=F32)
        values = rest[...] + tile4(late)
        first = lax.broadcasted_iota(jnp.int32, (8, 128), 0) == 0
        for c in range(8):
            message[c, 0:8] = pack(values[32 * c : 32 * c + 32], small)
            message[c, 8:16] = jnp.where(first, gain, row_sums[c])

    @pl.when(jnp.logical_not(has_fresh))
    def _():
        for c in range(8):
            message[c, 0:8] = pack(rest[32 * c : 32 * c + 32], small)
            message[c, 8:16] = jnp.zeros((8, 128), F32)

    for k in range(1, 8):
        other = (col + k) % 8
        pltpu.make_async_remote_copy(
            message.at[other], arrived.at[k - 1], qsend_sem.at[0], q_sem.at[0],
            device_id=(row, other), device_id_type=MESH,
        ).start()
    total = message[col]
    wait_for(arrived, q_sem.at[0])
    for k in range(7):
        total = total + arrived[k]
    gain = tile4(total[8:16])[0:1]
    values = jnp.concatenate([turn(total[0:8], 1 - g) for g in range(4)], axis=0)
    both = jnp.where(group == 0, fresh[...], jnp.where(group == 1, values, gain)).T
    out[0:32] = both[0:32]
    out[64:96] = both[64:96]
    out[32:64] = both[32:64] - both[64:96] * total[9:10, 0:32] + target_buf[...]

    wait_for(blocks.at[pl.ds(0, 63)], send_sem.at[0])
    wait_for(own_rows.at[:, pl.ds(32, 32)], psend_sem.at[0])
    wait_for(column.at[pl.ds(0, 8)], csend_sem.at[0])
    swap.wait_send()

    @pl.when(is_target)
    def _():
        wait_for(gathered.at[pl.ds(0, 15)], fsend_sem.at[0])

    @pl.when(jnp.logical_not(is_target))
    def _():
        wait_for(gathered.at[pl.ds(0, 16)], fsend_sem.at[0])

    wait_for(arrived, qsend_sem.at[0])


def local(policy_rows, action_rows, prev_values, action_costs, policy, target_costs, anchor):
    any_spec = pl.BlockSpec(memory_space=pl.ANY)
    dma = pltpu.SemaphoreType.DMA
    out = pl.pallas_call(
        kernel,
        out_shape=jax.ShapeDtypeStruct((96, 32), F32),
        in_specs=[any_spec] * 7,
        out_specs=pl.BlockSpec(memory_space=pltpu.VMEM),
        scratch_shapes=[
            pltpu.VMEM((32, 1024), F32),
            pltpu.VMEM((32, 8, 32), F32),
            pltpu.VMEM((1, 32), jnp.int32),
            pltpu.VMEM((32, 32), F32),
            pltpu.VMEM((1, 1), jnp.int32),
            pltpu.VMEM((64, 32, 1024), BF16),
            pltpu.VMEM((64, 64, 1024), BF16),
            pltpu.VMEM((2, 256, 8, 1024), BF16),
            pltpu.VMEM((16, 32, 1024), BF16),
            pltpu.VMEM((256, 1024), BF16),
            pltpu.VMEM((256, 128), F32),
            pltpu.VMEM((256, 128), F32),
            pltpu.VMEM((32, 128), F32),
            pltpu.VMEM((32, 128), F32),
            pltpu.VMEM((32, 128), F32),
            pltpu.VMEM((32, 128), F32),
            pltpu.VMEM((8, 128), F32),
            pltpu.VMEM((32, 8, 128), F32),
            pltpu.VMEM((1024, 128), BF16),
            pltpu.VMEM((8, 8, 128), F32),
            pltpu.VMEM((8, 16, 128), F32),
            pltpu.VMEM((7, 16, 128), F32),
            dma((5,)), dma((16,)), dma((16,)), dma((8,)), dma((128,)), dma((2,)), dma((1,)), dma((1,)), dma((1,)),
            dma((1,)), dma((1,)), dma((1,)), dma((1,)), dma((1,)), dma((1,)),
        ],
        compiler_params=pltpu.CompilerParams(
            collective_id=0, has_side_effects=True, vmem_limit_bytes=60 * 1024 * 1024
        ),
    )(
        policy_rows,
        action_rows.reshape(action_rows.shape[0], 16, 1024),
        prev_values,
        action_costs,
        policy.reshape(1, 32),
        target_costs,
        anchor.reshape(1, 1),
    )
    return out[0:32] - out[64:96], out[32:64] - out[64:96]


def solution(mesh):
    in_specs = (
        P(("row", "col"), None),
        P("row", None, "col", None),
        P(None, ("row", "col")),
        P(None, None, ("row", "col")),
        P(("row", "col")),
        P(None, ("row", "col")),
        P(),
    )
    out_specs = (P(None, ("row", "col")), P(None, ("row", "col")))
    return jax.shard_map(local, mesh=mesh, in_specs=in_specs, out_specs=out_specs, check_vma=False)
```
